32 devices in a mesh: rows: 16 (over z, y, core), cent: 2 (over x).
Axes of the slice: x: 2, y: 2, z: 4, core: 2. Of those that a mesh axis runs over, the one named last changes fastest.
Arguments:
- vectors: bfloat16 [32768, 1024], P('rows'), may hold values from -40 to 40
- centroids: bfloat16 [1024, 4096], P('rows', 'cent'), may hold values from -8 to 8
Outputs:
- centroid_sums: float32 [1024, 4096], P('rows', 'cent')
The draws below stay inside these ranges and needn't reach their ends.
All inputs are finite; a program needn't handle non-finite values.
Results may differ from the reference program's by a relative error of at most 0.0017.
Values may be sent and summed in bfloat16 or wider, within the bound.
A program may use at most 64 MiB of HBM per device.

```python
import math
import jax
import jax.numpy as jnp
from jax import lax

D = 1024
K = 4096
ITERS = 3
N = 32768


def column_norms(key):
    return jnp.exp(jax.random.uniform(jax.random.fold_in(key, 13), (K,), jnp.float32, math.log(0.5), math.log(2.0)))


def centroid_table(key):
    base = jnp.clip(jax.random.normal(jax.random.fold_in(key, 11), (D, K), jnp.float32), -4.0, 4.0)
    return base * column_norms(key)[None, :]


def draw_centroids(key, part):
    return centroid_table(key).astype(jnp.bfloat16)


def draw_vectors(key, part):
    base = jnp.clip(jax.random.normal(jax.random.fold_in(key, 23), (N, D), jnp.float32), -6.0, 6.0)
    return jnp.clip(base, -40.0, 40.0).astype(jnp.bfloat16)


def setup_inputs(seed: int = 0) -> dict:
    seeds = jax.random.split(jax.random.key(seed), 3)
    vectors = draw_vectors(jax.random.fold_in(seeds[2], 71), 0)
    centroids = draw_centroids(jax.random.fold_in(seeds[2], 71), 0)
    return {"vectors": vectors, "centroids": centroids}


sharpness = 3.0

def reference(vectors, centroids):
    scores = jnp.dot(vectors, centroids, preferred_element_type=jnp.float32) * (sharpness / math.sqrt(D))
    row_top = lax.optimization_barrier(jnp.max(scores, axis=1, keepdims=True))
    numerator = jnp.exp(scores - row_top)
    balanced = numerator / lax.optimization_barrier(jnp.sum(numerator, axis=1, keepdims=True))
    target = N / K
    for iteration in range(ITERS):
        column_mass = lax.optimization_barrier(jnp.sum(balanced, axis=0))
        column_scale = target / column_mass
        balanced = balanced * column_scale[None, :]
        balanced = balanced / lax.optimization_barrier(jnp.sum(balanced, axis=1, keepdims=True))
    weights = balanced.astype(jnp.bfloat16)
    summed = lax.dot_general(vectors, weights, (((0,), (0,)), ((), ())), preferred_element_type=jnp.float32)
    return summed * (K / N)
```

```python
import functools
import math

import jax
import jax.numpy as jnp
from jax import lax
from jax.experimental import pallas as pl
from jax.experimental.pallas import tpu as pltpu
from jax.sharding import PartitionSpec as P

ITERS = 3
SHARPNESS = 3.0
VECTOR_BOUND = 40.0
MESH = pl.DeviceIdType.MESH
LANES = 128
SHARES = 2
f32, bf16 = jnp.float32, jnp.bfloat16


def position_of(chip, chips):
    far, near = chip // 2, chip % 2
    return far + near * (chips - 1 - 2 * far)


def chip_at(place, chips):
    near = place // (chips // 2)
    far = place + near * (chips - 1 - 2 * place)
    return far * 2 + near


def plan(ring, rows, width, depth, cols):
    chips, half, block = ring // 2, cols // 2, 2 * depth
    chunk = min(256, half)
    spans = 2 if half >= 2 * chunk else 1
    return dict(
        chips=chips, half=half, block=block, chunk=chunk, spans=spans, chunks=half // chunk,
        pieces=half // spans // chunk, tile=min(1024, 2 * rows), steps=chips // 2,
        lots=max(1, half // 2 // LANES), wide=block % LANES == 0)


def encode(value):
    square = value * value
    return (square * (value * jnp.abs(value))).astype(bf16)


def decode(code):
    code = code.astype(f32)
    root = lax.rsqrt(lax.rsqrt(jnp.abs(code)))
    return jnp.where(code < 0, -root, root)


def kernel(ring, groups, total_rows, columns_total, vec_ref, cen_ref, out_ref, cen_full, vec_all, vec_t, bal, wts, acc, cen_t,
           top_s, sum_s, scale_s, row_acc, col_b, col_acc, row_x, col_x, rs_out, rs_in, last_in, own_in,
           ag_send, ag_recv, pair_send, pair_recv, vec_sem, row_send, row_recv, col_send, col_recv,
           rs_send, rs_recv, last_send, last_recv, own_sem):
    rows, width = vec_ref.shape
    depth, cols = cen_ref.shape
    p = plan(ring, rows, width, depth, cols)
    chips, half, block, chunk = p["chips"], p["half"], p["block"], p["chunk"]
    spans, pieces, tile, steps, lots = p["spans"], p["pieces"], p["tile"], p["steps"], p["lots"]
    chunks, wide = p["chunks"], p["wide"]
    both = 2 * rows
    strips = both // LANES
    per_share = strips // SHARES

    me = lax.axis_index("rows")
    cent = lax.axis_index("cent")
    chip, core = me // 2, me % 2
    other = 1 - core
    partner = chip * 2 + other
    pos = position_of(chip, chips)
    following = chip_at((pos + 1) % chips, chips)
    previous = chip_at((pos + chips - 1) % chips, chips)
    neighbours = (following, previous)

    def chip_behind(way, distance):
        where = (pos + 2 * chips - distance) % chips if way == 0 else (pos + distance) % chips
        return chip_at(where, chips)

    def remote(source, target, send, recv, device):
        return pltpu.make_async_remote_copy(
            src_ref=source, dst_ref=target, send_sem=send, recv_sem=recv, device_id=device, device_id_type=MESH)

    barrier = pltpu.get_barrier_semaphore()

    def greet(o, carry):
        pl.semaphore_signal(barrier, inc=1, device_id={"rows": (me + o) % ring}, device_id_type=MESH)
        return carry

    lax.fori_loop(1, ring, greet, 0)
    for o in range(1, groups):
        for row in (me, partner):
            pl.semaphore_signal(
                barrier, inc=1, device_id={"rows": row, "cent": (cent + o) % groups}, device_id_type=MESH)

    mine = pl.ds(pl.multiple_of(me * depth, depth), depth)
    my_rows = pl.ds(pl.multiple_of(core * rows, rows), rows)
    cen_full[mine, :] = cen_ref[:, pl.ds(pl.multiple_of(core * half, LANES), half)]
    vec_local = pltpu.make_async_copy(vec_ref, vec_all.at[my_rows, :], vec_sem.at[2])
    vec_local.start()
    pl.semaphore_wait(barrier, ring - 1 + 2 * (groups - 1))

    def piece_lanes(piece):
        return pl.ds(pl.multiple_of(piece * chunk, chunk), chunk)

    def own_copy(way, h, piece):
        view = cen_ref.at[:, pl.ds(pl.multiple_of(h * half + piece * chunk, LANES), chunk)]
        return remote(view, cen_full.at[mine, piece_lanes(piece)], ag_send.at[way, 0, h, piece],
                      ag_recv.at[way, 0, core, piece], {"rows": neighbours[way] * 2 + h})

    def pair_copy(piece):
        view = cen_ref.at[:, pl.ds(pl.multiple_of(other * half + piece * chunk, LANES), chunk)]
        return remote(view, cen_full.at[mine, piece_lanes(piece)], pair_send.at[piece], pair_recv.at[piece],
                      {"rows": partner})

    def gather_view(way, distance, sub, piece):
        start = (chip_behind(way, distance) * 2 + sub) * depth
        return cen_full.at[pl.ds(pl.multiple_of(start, depth), depth), piece_lanes(piece)]

    def gather_copy(way, step, sub, piece):
        view = gather_view(way, step, sub, piece)
        return remote(view, view, ag_send.at[way, step, sub, piece], ag_recv.at[way, step, sub, piece],
                      {"rows": neighbours[way] * 2 + core})

    def gather_arrival(way, step, sub, piece):
        view = gather_view(way, step + 1, sub, piece)
        return remote(view, view, ag_send.at[way, step, sub, piece], ag_recv.at[way, step, sub, piece],
                      {"rows": neighbours[way] * 2 + core})

    def forward(step, piece):
        for way in range(2):
            gather_arrival(way, step - 1, way, piece).wait_recv()
            gather_copy(way, step, way, piece).start()

        @pl.when(step < steps - 1)
        def _():
            for way in range(2):
                gather_arrival(way, step - 1, 1 - way, piece).wait_recv()
                gather_copy(way, step, 1 - way, piece).start()

    def forward_all(span, e):
        forward(1 + e // pieces, span * pieces + e % pieces)

    events = (steps - 1) * pieces

    def start_span(span):
        for q in range(pieces):
            piece = span * pieces + q
            for way in range(2):
                for h in range(2):
                    own_copy(way, h, piece).start()
            pair_copy(piece).start()

    def finish_span(span):
        for q in range(pieces):
            piece = span * pieces + q
            pair_copy(piece).wait_recv()
            for way in range(2):
                gather_arrival(way, steps - 2, 1 - way, piece).wait_recv()
                gather_arrival(way, steps - 1, way, piece).wait_recv()

    start_span(0)
    vec_copy = remote(vec_ref, vec_all.at[my_rows, :], vec_sem.at[0], vec_sem.at[1], {"rows": partner})
    vec_copy.start()

    turn_tile = 256

    def turn_rows(first):
        def turn(t, carry):
            at = pl.ds(pl.multiple_of(first + t * turn_tile, turn_tile), turn_tile)
            vec_t[:, at] = vec_all[at, :].T
            return carry

        lax.fori_loop(0, rows // turn_tile, turn, 0)

    vec_local.wait()
    turn_rows(core * rows)

    def forward_first(e, carry):
        forward_all(0, e)
        return carry

    lax.fori_loop(0, events, forward_first, 0)
    if spans > 1:
        start_span(1)
    vec_copy.wait_recv()
    turn_rows(other * rows)
    finish_span(0)

    scale = SHARPNESS / math.sqrt(width)
    tiles = both // tile
    units = chunks // spans * tiles

    def unit(u, carry):
        k, t = u // tiles, u % tiles
        columns = pl.ds(pl.multiple_of(k * chunk, chunk), chunk)
        at = pl.ds(pl.multiple_of(t * tile, tile), tile)

        @pl.when(t == 0)
        def _():
            cen_t[...] = cen_full[:, columns].T

        s = jnp.dot(cen_t[...], vec_t[:, at], preferred_element_type=f32) * scale
        top = s[0:8]
        for q in range(1, chunk // 8):
            top = jnp.maximum(top, s[q * 8:(q + 1) * 8])
        top = jnp.max(top, axis=0, keepdims=True)
        e = jnp.exp(s - top)
        total = e[0:8]
        for q in range(1, chunk // 8):
            total = total + e[q * 8:(q + 1) * 8]
        bal[columns, at] = e
        top_s[pl.ds(k, 1), at] = top
        sum_s[pl.ds(k, 1), at] = jnp.sum(total, axis=0, keepdims=True)
        return carry

    def unit_and_forward(u, carry):
        unit(u, carry)
        forward_all(1, u)
        return carry

    if spans > 1:
        shared = min(events, units)
        lax.fori_loop(0, shared, unit_and_forward, 0)
        lax.fori_loop(shared, units, unit, 0)

        def forward_rest(e, carry):
            forward_all(1, e)
            return carry

        lax.fori_loop(shared, events, forward_rest, 0)
        finish_span(1)
        lax.fori_loop(units, 2 * units, unit, 0)
    else:
        lax.fori_loop(0, units, unit, 0)

    partners = [(o, f) for o in range(groups) for f in range(2) if o + f > 0]

    def share_lanes(share):
        return slice(share * per_share * LANES, (share + 1) * per_share * LANES)

    def row_copy(turn_, share, o, f, both_rows):
        slot = o * 2 + f
        here = slice(0, 2) if both_rows else slice(0, 1)
        lanes = share_lanes(share)
        return remote(row_x.at[turn_, 0, here, lanes], row_x.at[turn_, slot, here, lanes],
                      row_send.at[turn_, share, slot], row_recv.at[turn_, share, slot],
                      {"rows": partner if f else me, "cent": (cent + o) % groups})

    def send_rows(turn_, share):
        for o, f in partners:
            row_copy(turn_, share, o, f, turn_ == 0).start()

    def receive_rows(turn_, share):
        for o, f in partners:
            row_copy(turn_, share, o, f, turn_ == 0).wait_recv()

    slots = [0] + [o * 2 + f for o, f in partners]

    for share in range(SHARES):
        lanes = share_lanes(share)
        tops = [top_s[k:k + 1, lanes] for k in range(chunks)]
        top = functools.reduce(jnp.maximum, tops)
        row_x[0, 0, 0:1, lanes] = top
        row_x[0, 0, 1:2, lanes] = functools.reduce(
            jnp.add, [sum_s[k:k + 1, lanes] * jnp.exp(tops[k] - top) for k in range(chunks)])
        send_rows(0, share)

    def softmax_rows(share):
        receive_rows(0, share)
        lanes = share_lanes(share)
        tops = [row_x[0, o, 0:1, lanes] for o in slots]
        top = functools.reduce(jnp.maximum, tops)
        total = functools.reduce(jnp.add, [row_x[0, o, 1:2, lanes] * jnp.exp(m - top) for o, m in zip(slots, tops)])
        for k in range(chunks):
            scale_s[k:k + 1, lanes] = jnp.exp(top_s[k:k + 1, lanes] - top) / total

    def balance_rows(turn_, share):
        receive_rows(turn_, share)
        lanes = share_lanes(share)
        scale_s[0:1, lanes] = 1.0 / functools.reduce(jnp.add, [row_x[turn_, o, 0:1, lanes] for o in slots])

    def strip(share, j):
        start = (share * per_share + j) * LANES
        return slice(start, start + LANES)

    def column_part(share, lot, scale_row):
        r = [jnp.broadcast_to(scale_s[scale_row:scale_row + 1, strip(share, j)], (8, LANES)) for j in range(per_share)]

        def body(t, carry):
            at = pl.ds(pl.multiple_of(lot * chunk + t * 8, 8), 8)
            sums = [None] * 4
            for j in range(per_share):
                b = bal[at, strip(share, j)] * r[j]
                sums[j % 4] = b if sums[j % 4] is None else sums[j % 4] + b
            total = (sums[0] + sums[1]) + (sums[2] + sums[3])
            col_acc[at, :] = total if share == 0 else col_acc[at, :] + total
            return carry

        lax.fori_loop(0, chunk // 8, body, 0, unroll=2)

    def row_part(share, lot, scaled_row):
        if scaled_row is not None:
            r = [jnp.broadcast_to(scale_s[scaled_row:scaled_row + 1, strip(share, j)], (8, LANES))
                 for j in range(per_share)]

        def body(t, sums):
            at = pl.ds(pl.multiple_of(lot * chunk + t * 8, 8), 8)
            c = col_b[at, :]
            new = []
            for j in range(per_share):
                b = bal[at, strip(share, j)]
                if scaled_row is not None:
                    b = b * r[j]
                b = b * c
                if scaled_row is not None:
                    bal[at, strip(share, j)] = b
                new.append(sums[j] + b)
            return tuple(new)

        if lot == 0:
            sums = tuple(jnp.zeros((8, LANES), f32) for _ in range(per_share))
        else:
            sums = tuple(row_acc[:, strip(share, j)] for j in range(per_share))
        sums = lax.fori_loop(0, chunk // 8, body, sums, unroll=2)
        for j in range(per_share):
            row_acc[:, strip(share, j)] = sums[j]

    def col_copy(it, lot, o):
        lanes = slice(lot * chunk, (lot + 1) * chunk)
        return remote(col_x.at[it, 0, :, lanes], col_x.at[it, o, :, lanes], col_send.at[it, lot, o],
                      col_recv.at[it, lot, o], {"rows": (chip + o) % chips * 2 + core})

    target = total_rows / columns_total

    def send_column(it, lot):
        lanes = slice(lot * chunk, (lot + 1) * chunk)
        col_x[it, 0, :, lanes] = jnp.sum(col_acc[lanes, :].T, axis=0, keepdims=True)

        def send(o, carry):
            col_copy(it, lot, o).start()
            return carry

        lax.fori_loop(1, chips, send, 0)

    def receive_column(it, lot, scale_before):
        lanes = slice(lot * chunk, (lot + 1) * chunk)

        def receive(o, carry):
            col_copy(it, lot, o).wait_recv()
            return carry + col_x[it, o, :, lanes]

        mass = lax.fori_loop(1, chips, receive, col_x[it, 0, :, lanes])
        c = target / mass
        col_b[lanes, :] = jnp.broadcast_to(c, (LANES, chunk)).T

    for it in range(ITERS):
        for share in range(SHARES):
            if it == 0:
                softmax_rows(share)
            else:
                balance_rows(it, share)
            for lot in range(chunks):
                column_part(share, lot, lot if it == 0 else 0)
                if share == SHARES - 1:
                    send_column(it, lot)
        for lot in range(chunks):
            receive_column(it, lot, None)
            for share in range(SHARES):
                row_part(share, lot, lot if it == 0 else None)
                if lot == chunks - 1:
                    lanes = share_lanes(share)
                    row_x[it + 1, 0, 0:1, lanes] = jnp.sum(row_acc[:, lanes], axis=0, keepdims=True)
                    send_rows(it + 1, share)

    def weigh(share):
        def body(t, carry):
            at = pl.ds(pl.multiple_of(t * 16, 16), 16)
            c = col_b[at, :]
            for j in range(per_share):
                wts[at, strip(share, j)] = (bal[at, strip(share, j)] * c * scale_s[0:1, strip(share, j)]).astype(bf16)
            return carry

        lax.fori_loop(0, half // 16, body, 0)

    for share in range(SHARES):
        balance_rows(ITERS, share)
        weigh(share)

    way_cols = half // 2
    limit = VECTOR_BOUND * columns_total
    lift = 2.0 ** math.floor(math.log2(3.0e9 / limit))
    factor = columns_total / total_rows * lift
    mt = min(256, way_cols)

    def block_rows(chip_):
        return pl.ds(pl.multiple_of(chip_ * block, block), block)

    def produce(j, carry):
        for way in range(2):
            pair = [chip_behind(way, 2 * j + 1), chip_behind(way, 2 * j + 2)]
            right = jnp.concatenate([vec_all[:, block_rows(q)] for q in pair], axis=1)
            for m in range(way_cols // mt):
                at = slice(way * way_cols + m * mt, way * way_cols + (m + 1) * mt)
                s = (jnp.dot(wts[at, :], right, preferred_element_type=f32) * factor).T
                for i, q in enumerate(pair):
                    acc[block_rows(q), at] = s[i * block:(i + 1) * block]
        return carry

    def produce_all():
        dt = min(256, width)

        def body(t, carry):
            at = pl.ds(pl.multiple_of(t * dt, dt), dt)
            for m in range(half // mt):
                lanes = slice(m * mt, (m + 1) * mt)
                acc[at, lanes] = (jnp.dot(wts[lanes, :], vec_all[:, at], preferred_element_type=f32) * factor).T
            return carry

        lax.fori_loop(0, width // dt, body, 0)

    lw = way_cols // lots if way_cols % LANES == 0 else way_cols

    def lot_lanes(way, lot):
        return slice(way * way_cols + lot * lw, way * way_cols + (lot + 1) * lw)

    lot_count = way_cols // lw

    def sum_copy(way, lot, step):
        lanes = lot_lanes(way, lot)
        return remote(rs_out.at[step, :, lanes], rs_in.at[step, :, lanes], rs_send.at[step, way, lot],
                      rs_recv.at[step, way, lot], {"rows": neighbours[way] * 2 + core})

    def last_copy(way, lot, a):
        lanes = lot_lanes(way, lot)
        return remote(rs_out.at[chips - 2, a * depth:(a + 1) * depth, lanes], last_in.at[core, :, lanes],
                      last_send.at[a, way, lot], last_recv.at[core, way, lot], {"rows": neighbours[way] * 2 + a})

    def last_arrival(way, lot, h):
        lanes = lot_lanes(way, lot)
        return remote(rs_out.at[chips - 2, 0:depth, lanes], last_in.at[h, :, lanes],
                      last_send.at[0, way, lot], last_recv.at[h, way, lot], {"rows": neighbours[way] * 2 + core})

    def sum_step(step, first=False, last=False):
        for lot in range(lot_count):
            for way in range(2):
                lanes = lot_lanes(way, lot)
                value = acc[block_rows(chip_behind(way, step + 1)), lanes]
                if not first:
                    sum_copy(way, lot, step - 1).wait_recv()
                    value = value + decode(rs_in[step - 1, :, lanes])
                rs_out[step, :, lanes] = encode(value)
                if last:
                    for a in range(2):
                        last_copy(way, lot, a).start()
                else:
                    sum_copy(way, lot, step).start()

    if wide:
        produce(0, 0)
    else:
        produce_all()
    sum_step(0, first=True)

    def double_step(j, carry):
        if wide:
            produce(j, 0)
        sum_step(2 * j - 1)
        sum_step(2 * j)
        return carry

    lax.fori_loop(1, chips // 2 - 1, double_step, 0)
    if wide:
        produce(chips // 2 - 1, 0)
    own_copy_sum = remote(acc.at[pl.ds(pl.multiple_of(partner * depth, depth), depth), :], own_in,
                          own_sem.at[0], own_sem.at[1], {"rows": partner})
    own_copy_sum.start()
    sum_step(chips - 3)
    sum_step(chips - 2, last=True)

    own_copy_sum.wait_recv()
    for lot in range(lot_count):
        for way in range(2):
            lanes = lot_lanes(way, lot)
            for h, extra in ((core, acc[mine, lanes]), (other, own_in[:, lanes])):
                last_arrival(way, lot, h).wait_recv()
                value = decode(last_in[h, :, lanes]) + extra
                start = h * half + lanes.start
                out_ref[:, pl.ds(pl.multiple_of(start, lw if lw < LANES else LANES), lw)] = value * (1.0 / lift)

    for piece in range(spans * pieces):
        pair_copy(piece).wait_send()
        for way in range(2):
            for h in range(2):
                own_copy(way, h, piece).wait_send()

    def drain_gather(step, carry):
        for piece in range(spans * pieces):
            for way in range(2):
                gather_copy(way, step, way, piece).wait_send()

                @pl.when(step < steps - 1)
                def _():
                    gather_copy(way, step, 1 - way, piece).wait_send()
        return carry

    lax.fori_loop(1, steps, drain_gather, 0)
    vec_copy.wait_send()
    for turn_ in range(ITERS + 1):
        for share in range(SHARES):
            for o, f in partners:
                row_copy(turn_, share, o, f, turn_ == 0).wait_send()

    def drain_columns(o, carry):
        for it in range(ITERS):
            for lot in range(chunks):
                col_copy(it, lot, o).wait_send()
        return carry

    lax.fori_loop(1, chips, drain_columns, 0)

    def drain_sums(step, carry):
        for lot in range(lot_count):
            for way in range(2):
                sum_copy(way, lot, step).wait_send()
        return carry

    lax.fori_loop(0, chips - 2, drain_sums, 0)
    for lot in range(lot_count):
        for way in range(2):
            for a in range(2):
                last_copy(way, lot, a).wait_send()
    own_copy_sum.wait_send()


def solution(mesh):
    ring, groups = mesh.shape["rows"], mesh.shape["cent"]

    def on_device(vectors, centroids):
        rows, width = vectors.shape
        depth, cols = centroids.shape
        p = plan(ring, rows, width, depth, cols)
        chips, half, block, lots = p["chips"], p["half"], p["block"], p["lots"]
        both = 2 * rows
        pieces = p["spans"] * p["pieces"]
        dma = pltpu.SemaphoreType.DMA
        vmem = pltpu.VMEM
        return pl.pallas_call(
            functools.partial(kernel, ring, groups, rows * ring, cols * groups),
            out_shape=jax.ShapeDtypeStruct((depth, cols), f32),
            in_specs=[pl.BlockSpec(memory_space=pltpu.VMEM)] * 2,
            out_specs=pl.BlockSpec(memory_space=pltpu.VMEM),
            scratch_shapes=[
                vmem((width, half), bf16),
                vmem((both, width), bf16),
                vmem((width, both), bf16),
                vmem((half, both), f32),
                vmem((half, both), bf16),
                vmem((width, half), f32),
                vmem((p["chunk"], width), bf16),
                vmem((max(8, p["chunks"]), both), f32),
                vmem((max(8, p["chunks"]), both), f32),
                vmem((max(8, p["chunks"]), both), f32),
                vmem((8, both), f32),
                vmem((half, LANES), f32),
                vmem((half, LANES), f32),
                vmem((ITERS + 1, 2 * groups, 2, both), f32),
                vmem((ITERS, chips, 1, half), f32),
                vmem((chips - 1, block, half), bf16),
                vmem((chips - 2, block, half), bf16),
                vmem((2, depth, half), bf16),
                vmem((depth, half), f32),
                dma((2, p["steps"], 2, pieces)),
                dma((2, p["steps"], 2, pieces)),
                dma((pieces,)),
                dma((pieces,)),
                dma((3,)),
                dma((ITERS + 1, SHARES, 2 * groups)),
                dma((ITERS + 1, SHARES, 2 * groups)),
                dma((ITERS, p["chunks"], chips)),
                dma((ITERS, p["chunks"], chips)),
                dma((chips - 2, 2, lots)),
                dma((chips - 2, 2, lots)),
                dma((2, 2, lots)),
                dma((2, 2, lots)),
                dma((2,)),
            ],
            compiler_params=pltpu.CompilerParams(
                collective_id=0, has_side_effects=True, vmem_limit_bytes=66 * 1000 * 1000),
        )(vectors, centroids)

    return jax.shard_map(
        on_device,
        mesh=mesh,
        in_specs=(P("rows", None), P("rows", "cent")),
        out_specs=P("rows", "cent"),
        check_vma=False,
    )
```

```python
import functools
import math

import jax
import jax.numpy as jnp
from jax import lax
from jax.experimental import pallas as pl
from jax.experimental.pallas import tpu as pltpu
from jax.sharding import PartitionSpec as P

ITERS = 3
SHARPNESS = 3.0
VECTOR_BOUND = 40.0
MESH = pl.DeviceIdType.MESH
LANES = 128
SHARES = 2
f32, bf16 = jnp.float32, jnp.bfloat16


def position_of(chip, chips):
    far, near = chip // 2, chip % 2
    return far + near * (chips - 1 - 2 * far)


def chip_at(place, chips):
    near = place // (chips // 2)
    far = place + near * (chips - 1 - 2 * place)
    return far * 2 + near


def plan(ring, rows, width, depth, cols):
    chips, half, block = ring // 2, cols // 2, 2 * depth
    chunk = min(256, half)
    return dict(
        chips=chips, half=half, block=block, chunk=chunk, chunks=half // chunk, tile=min(1024, 2 * rows),
        steps=chips // 2, lots=max(1, half // 2 // (2 * LANES)), wide=block % LANES == 0 and chips == 8)


def encode(value):
    square = value * value
    return (square * (value * jnp.abs(value))).astype(bf16)


def decode(code):
    code = code.astype(f32)
    root = lax.rsqrt(lax.rsqrt(jnp.abs(code)))
    return jnp.where(code < 0, -root, root)


def kernel(ring, groups, total_rows, columns_total, vec_hbm, cen_hbm, out_ref, cen_own, cen_full, vec_all, vec_t, bal, wts, acc, cen_t,
           top_s, sum_s, scale_s, row_acc, col_b, col_acc, row_x, col_x, rs_out, rs_in, last_in, own_in,
           ag_send, ag_recv, pair_sem, vec_sem, row_send, row_recv, col_send, col_recv,
           rs_send, rs_recv, last_send, last_recv, own_sem):
    rows, width = vec_hbm.shape
    depth, cols = cen_hbm.shape
    p = plan(ring, rows, width, depth, cols)
    chips, half, block, chunk = p["chips"], p["half"], p["block"], p["chunk"]
    tile, steps, lots = p["tile"], p["steps"], p["lots"]
    chunks, wide = p["chunks"], p["wide"]
    both = 2 * rows
    strips = both // LANES
    per_share = strips // SHARES

    me = lax.axis_index("rows")
    cent = lax.axis_index("cent")
    chip, core = me // 2, me % 2
    other = 1 - core
    partner = chip * 2 + other
    pos = position_of(chip, chips)
    following = chip_at((pos + 1) % chips, chips)
    previous = chip_at((pos + chips - 1) % chips, chips)
    neighbours = (following, previous)

    def chip_behind(way, distance):
        where = (pos + 2 * chips - distance) % chips if way == 0 else (pos + distance) % chips
        return chip_at(where, chips)

    def remote(source, target, send, recv, device):
        return pltpu.make_async_remote_copy(
            src_ref=source, dst_ref=target, send_sem=send, recv_sem=recv, device_id=device, device_id_type=MESH)

    mine = pl.ds(pl.multiple_of(me * depth, depth), depth)
    my_rows = pl.ds(pl.multiple_of(core * rows, rows), rows)
    cen_local = pltpu.make_async_copy(cen_hbm, cen_own, vec_sem.at[3])
    cen_local.start()
    vec_local = pltpu.make_async_copy(vec_hbm, vec_all.at[my_rows, :], vec_sem.at[2])
    vec_local.start()

    barrier = pltpu.get_barrier_semaphore()

    def greet(o, carry):
        pl.semaphore_signal(barrier, inc=1, device_id={"rows": (me + o) % ring}, device_id_type=MESH)
        return carry

    lax.fori_loop(1, ring, greet, 0)
    for o in range(1, groups):
        for row in (me, partner):
            pl.semaphore_signal(
                barrier, inc=1, device_id={"rows": row, "cent": (cent + o) % groups}, device_id_type=MESH)

    cen_local.wait()
    cen_full[mine, :] = cen_own[:, pl.ds(pl.multiple_of(core * half, LANES), half)]
    pl.semaphore_wait(barrier, ring - 1 + 2 * (groups - 1))

    def half_view(h):
        return cen_own.at[:, pl.ds(pl.multiple_of(h * half, LANES), half)]

    def own_copy(way, h):
        return remote(half_view(h), cen_full.at[mine, :], ag_send.at[way, 0, h],
                      ag_recv.at[way, 0, core], {"rows": neighbours[way] * 2 + h})

    pair_copy = remote(half_view(other), cen_full.at[mine, :], pair_sem.at[0], pair_sem.at[1], {"rows": partner})

    def gather_view(way, distance, sub):
        start = (chip_behind(way, distance) * 2 + sub) * depth
        return cen_full.at[pl.ds(pl.multiple_of(start, depth), depth), :]

    def gather_copy(way, step, sub):
        view = gather_view(way, step, sub)
        return remote(view, view, ag_send.at[way, step, sub], ag_recv.at[way, step, sub],
                      {"rows": neighbours[way] * 2 + core})

    def gather_arrival(way, step, sub):
        view = gather_view(way, step + 1, sub)
        return remote(view, view, ag_send.at[way, step, sub], ag_recv.at[way, step, sub],
                      {"rows": neighbours[way] * 2 + core})

    def forward(step, carry):
        for turn_ in range(2):
            for way in range(2):
                sub = way if turn_ == 0 else 1 - way
                gather_arrival(way, step - 1, sub).wait_recv()
                gather_copy(way, step, sub).start()
        return carry

    def forward_last():
        for way in range(2):
            gather_arrival(way, steps - 2, way).wait_recv()
            gather_copy(way, steps - 1, way).start()

    for h in range(2):
        for way in range(2):
            own_copy(way, h).start()
    pair_copy.start()
    vec_local.wait()
    vec_copy = remote(vec_all.at[my_rows, :], vec_all.at[my_rows, :], vec_sem.at[0], vec_sem.at[1], {"rows": partner})
    vec_copy.start()

    turn_tile = 256

    def turn_rows(first):
        def turn(t, carry):
            at = pl.ds(pl.multiple_of(first + t * turn_tile, turn_tile), turn_tile)
            vec_t[:, at] = vec_all[at, :].T
            return carry

        lax.fori_loop(0, rows // turn_tile, turn, 0)

    turn_rows(core * rows)

    scale = SHARPNESS / math.sqrt(width)

    def block_rows(chip_):
        return pl.ds(pl.multiple_of(chip_ * block, block), block)

    def score_pass(blocks, first, final, begin=0, end=chunks):
        tile_here = tile if final else min(2 * tile, both)
        depth_here = width if blocks is None else len(blocks) * block

        def per_chunk(k, carry):
            columns = pl.ds(pl.multiple_of(k * chunk, chunk), chunk)
            if blocks is None:
                cen_t[...] = cen_full[:, columns].T
            else:
                cen_t[:, 0:depth_here] = jnp.concatenate([cen_full[block_rows(q), columns] for q in blocks], axis=0).T

            def per_tile(t, carry):
                at = pl.ds(pl.multiple_of(t * tile_here, tile_here), tile_here)
                if blocks is None:
                    right = vec_t[:, at]
                else:
                    right = jnp.concatenate([vec_t[block_rows(q), at] for q in blocks], axis=0)
                s = jnp.dot(cen_t[:, 0:depth_here], right, preferred_element_type=f32)
                if not first:
                    s = bal[columns, at] + s
                if not final:
                    bal[columns, at] = s
                    return carry
                s = s * scale
                top = s[0:8]
                for q in range(1, chunk // 8):
                    top = jnp.maximum(top, s[q * 8:(q + 1) * 8])
                top = jnp.max(top, axis=0, keepdims=True)
                e = jnp.exp(s - top)
                total = e[0:8]
                for q in range(1, chunk // 8):
                    total = total + e[q * 8:(q + 1) * 8]
                bal[columns, at] = e
                top_s[pl.ds(k, 1), at] = top
                sum_s[pl.ds(k, 1), at] = jnp.sum(total, axis=0, keepdims=True)
                return carry

            return lax.fori_loop(0, both // tile_here, per_tile, carry)

        lax.fori_loop(begin, end, per_chunk, 0)

    def wait_last():
        for way in range(2):
            gather_arrival(way, steps - 1, way).wait_recv()

    lax.fori_loop(1, steps - 1, forward, 0)
    pair_copy.wait_recv()
    vec_copy.wait_recv()
    turn_rows(other * rows)
    if wide:
        near = [chip, chip_behind(0, 1), chip_behind(1, 1), chip_behind(0, 2)]
        score_pass(near, True, False, 0, chunks // 2)
        forward_last()
        score_pass(near, True, False, chunks // 2, chunks)
        for way in range(2):
            gather_arrival(way, steps - 2, 1 - way).wait_recv()
        wait_last()
        score_pass([chip_behind(1, 2), chip_behind(0, 3), chip_behind(1, 3), chip_behind(0, 4)], False, True)
    else:
        forward_last()
        for way in range(2):
            gather_arrival(way, steps - 2, 1 - way).wait_recv()
        wait_last()
        score_pass(None, True, True)

    partners = [(o, f) for o in range(groups) for f in range(2) if o + f > 0]

    def share_lanes(share):
        return slice(share * per_share * LANES, (share + 1) * per_share * LANES)

    def row_copy(turn_, share, o, f, both_rows):
        slot = o * 2 + f
        here = slice(0, 2) if both_rows else slice(0, 1)
        lanes = share_lanes(share)
        return remote(row_x.at[turn_, 0, here, lanes], row_x.at[turn_, slot, here, lanes],
                      row_send.at[turn_, share, slot], row_recv.at[turn_, share, slot],
                      {"rows": partner if f else me, "cent": (cent + o) % groups})

    def send_rows(turn_, share):
        for o, f in partners:
            row_copy(turn_, share, o, f, turn_ == 0).start()

    def receive_rows(turn_, share):
        for o, f in partners:
            row_copy(turn_, share, o, f, turn_ == 0).wait_recv()

    slots = [0] + [o * 2 + f for o, f in partners]

    for share in range(SHARES):
        lanes = share_lanes(share)
        tops = [top_s[k:k + 1, lanes] for k in range(chunks)]
        top = functools.reduce(jnp.maximum, tops)
        row_x[0, 0, 0:1, lanes] = top
        row_x[0, 0, 1:2, lanes] = functools.reduce(
            jnp.add, [sum_s[k:k + 1, lanes] * jnp.exp(tops[k] - top) for k in range(chunks)])
        send_rows(0, share)

    def softmax_rows(share):
        receive_rows(0, share)
        lanes = share_lanes(share)
        tops = [row_x[0, o, 0:1, lanes] for o in slots]
        top = functools.reduce(jnp.maximum, tops)
        total = functools.reduce(jnp.add, [row_x[0, o, 1:2, lanes] * jnp.exp(m - top) for o, m in zip(slots, tops)])
        for k in range(chunks):
            scale_s[k:k + 1, lanes] = jnp.exp(top_s[k:k + 1, lanes] - top) / total

    def balance_rows(turn_, share):
        receive_rows(turn_, share)
        lanes = share_lanes(share)
        scale_s[0:1, lanes] = 1.0 / functools.reduce(jnp.add, [row_x[turn_, o, 0:1, lanes] for o in slots])

    def strip(share, j):
        start = (share * per_share + j) * LANES
        return slice(start, start + LANES)

    def column_part(share, lot, scale_row):
        r = [jnp.broadcast_to(scale_s[scale_row:scale_row + 1, strip(share, j)], (8, LANES)) for j in range(per_share)]

        def body(t, carry):
            at = pl.ds(pl.multiple_of(lot * chunk + t * 8, 8), 8)
            sums = [None] * 4
            for j in range(per_share):
                b = bal[at, strip(share, j)] * r[j]
                sums[j % 4] = b if sums[j % 4] is None else sums[j % 4] + b
            total = (sums[0] + sums[1]) + (sums[2] + sums[3])
            col_acc[at, :] = total if share == 0 else col_acc[at, :] + total
            return carry

        lax.fori_loop(0, chunk // 8, body, 0, unroll=4)

    def row_part(share, scaled):
        sums = tuple(jnp.zeros((8, LANES), f32) for _ in range(per_share))

        def span(first, count, scale_row, sums):
            if scaled:
                r = [jnp.broadcast_to(scale_s[scale_row:scale_row + 1, strip(share, j)], (8, LANES))
                     for j in range(per_share)]

            def body(t, sums):
                at = pl.ds(pl.multiple_of(first + t * 8, 8), 8)
                c = col_b[at, :]
                new = []
                for j in range(per_share):
                    b = bal[at, strip(share, j)]
                    if scaled:
                        b = b * r[j]
                    b = b * c
                    if scaled:
                        bal[at, strip(share, j)] = b
                    new.append(sums[j] + b)
                return tuple(new)

            return lax.fori_loop(0, count, body, sums, unroll=4)

        if scaled:
            for k in range(chunks):
                sums = span(k * chunk, chunk // 8, k, sums)
        else:
            sums = span(0, half // 8, 0, sums)
        for j in range(per_share):
            row_acc[:, strip(share, j)] = sums[j]

    def col_copy(it, o):
        return remote(col_x.at[it, 0], col_x.at[it, o], col_send.at[it, o], col_recv.at[it, o],
                      {"rows": (chip + o) % chips * 2 + core})

    target = total_rows / columns_total

    def send_column(it):
        col_x[it, 0] = jnp.sum(col_acc[...].T, axis=0, keepdims=True)

        def send(o, carry):
            col_copy(it, o).start()
            return carry

        lax.fori_loop(1, chips, send, 0)

    def receive_column(it):
        def receive(o, carry):
            col_copy(it, o).wait_recv()
            return carry + col_x[it, o]

        mass = lax.fori_loop(1, chips, receive, col_x[it, 0])
        col_b[...] = jnp.broadcast_to(target / mass, (LANES, half)).T

    for it in range(ITERS):
        for share in range(SHARES):
            if it == 0:
                softmax_rows(share)
            else:
                balance_rows(it, share)
            for lot in range(chunks):
                column_part(share, lot, lot if it == 0 else 0)
        send_column(it)
        receive_column(it)
        for share in range(SHARES):
            row_part(share, it == 0)
            lanes = share_lanes(share)
            row_x[it + 1, 0, 0:1, lanes] = jnp.sum(row_acc[:, lanes], axis=0, keepdims=True)
            send_rows(it + 1, share)

    def weigh(first, count):
        for share in range(SHARES):
            def body(t, carry):
                at = pl.ds(pl.multiple_of(first + t * 16, 16), 16)
                c = col_b[at, :]
                for j in range(per_share):
                    r = scale_s[0:1, strip(share, j)]
                    wts[at, strip(share, j)] = (bal[at, strip(share, j)] * c * r).astype(bf16)
                return carry

            lax.fori_loop(0, count // 16, body, 0)

    for share in range(SHARES):
        balance_rows(ITERS, share)

    way_cols = half // 2
    limit = VECTOR_BOUND * columns_total
    lift = 2.0 ** math.floor(math.log2(3.0e9 / limit))
    factor = columns_total / total_rows * lift
    lw = way_cols // lots

    def produce(way, lot, j):
        pair = [chip_behind(way, 2 * j + 1), chip_behind(way, 2 * j + 2)]
        right = jnp.concatenate([vec_all[:, block_rows(q)] for q in pair], axis=1)
        at = lot_lanes(way, lot)
        s = (jnp.dot(wts[at, :], right, preferred_element_type=f32) * factor).T
        for i, q in enumerate(pair):
            acc[block_rows(q), at] = s[i * block:(i + 1) * block]

    def produce_all():
        dt, mt = min(256, width), min(256, way_cols)

        def body(t, carry):
            at = pl.ds(pl.multiple_of(t * dt, dt), dt)
            for m in range(half // mt):
                lanes = slice(m * mt, (m + 1) * mt)
                acc[at, lanes] = (jnp.dot(wts[lanes, :], vec_all[:, at], preferred_element_type=f32) * factor).T
            return carry

        lax.fori_loop(0, width // dt, body, 0)

    def lot_lanes(way, lot):
        return slice(way * way_cols + lot * lw, way * way_cols + (lot + 1) * lw)

    lot_count = lots

    def sum_copy(way, lot, step):
        lanes = lot_lanes(way, lot)
        return remote(rs_out.at[step, :, lanes], rs_in.at[step, :, lanes], rs_send.at[step, way, lot],
                      rs_recv.at[step, way, lot], {"rows": neighbours[way] * 2 + core})

    def last_copy(way, lot, a):
        lanes = lot_lanes(way, lot)
        return remote(rs_out.at[chips - 2, a * depth:(a + 1) * depth, lanes], last_in.at[core, :, lanes],
                      last_send.at[a, way, lot], last_recv.at[core, way, lot], {"rows": neighbours[way] * 2 + a})

    def last_arrival(way, lot, h):
        lanes = lot_lanes(way, lot)
        return remote(rs_out.at[chips - 2, 0:depth, lanes], last_in.at[h, :, lanes],
                      last_send.at[0, way, lot], last_recv.at[h, way, lot], {"rows": neighbours[way] * 2 + core})

    def sum_step(step, first=False, last=False, before=None, after=None):
        for lot in range(lot_count):
            values = []
            for way in range(2):
                if before is not None:
                    before(way, lot)
                if not first:
                    sum_copy(way, lot, step - 1).wait_recv()
            for way in range(2):
                lanes = lot_lanes(way, lot)
                value = acc[block_rows(chip_behind(way, step + 1)), lanes]
                if not first:
                    value = value + decode(rs_in[step - 1, :, lanes])
                values.append(encode(value))
            for way in range(2):
                rs_out[step, :, lot_lanes(way, lot)] = values[way]
            for way in range(2):
                if last:
                    for a in range(2):
                        last_copy(way, lot, a).start()
                else:
                    sum_copy(way, lot, step).start()
            if after is not None:
                after(lot)

    if wide:
        def first_produce(way, lot):
            weigh(way * way_cols + lot * lw, lw)
            produce(way, lot, 0)

        sum_step(0, first=True, before=first_produce)
        for lot in range(lot_count):
            produce(0, lot, 1)
        sum_step(1, after=lambda lot: produce(1, lot, 1))

        def double_step(j, carry):
            sum_step(2 * j, after=lambda lot: produce(0, lot, j + 1))
            sum_step(2 * j + 1, after=lambda lot: produce(1, lot, j + 1))
            return carry

        lax.fori_loop(1, chips // 2 - 1, double_step, 0)
    else:
        weigh(0, half)
        produce_all()
        sum_step(0, first=True)

        def single_step(step, carry):
            sum_step(step)
            return carry

        lax.fori_loop(1, chips - 2, single_step, 0)
    own_copy_sum = remote(acc.at[pl.ds(pl.multiple_of(partner * depth, depth), depth), :], own_in,
                          own_sem.at[0], own_sem.at[1], {"rows": partner})
    own_copy_sum.start()
    sum_step(chips - 2, last=True)

    own_copy_sum.wait_recv()
    for lot in range(lot_count):
        for way in range(2):
            lanes = lot_lanes(way, lot)
            for h, extra in ((core, acc[mine, lanes]), (other, own_in[:, lanes])):
                last_arrival(way, lot, h).wait_recv()
                value = decode(last_in[h, :, lanes]) + extra
                start = h * half + lanes.start
                out_ref[:, pl.ds(pl.multiple_of(start, lw if lw < LANES else LANES), lw)] = value * (1.0 / lift)

    pair_copy.wait_send()
    for way in range(2):
        for h in range(2):
            own_copy(way, h).wait_send()

    def drain_gather(step, carry):
        for way in range(2):
            for sub in range(2):
                gather_copy(way, step, sub).wait_send()
        return carry

    lax.fori_loop(1, steps - 1, drain_gather, 0)
    for way in range(2):
        gather_copy(way, steps - 1, way).wait_send()
    vec_copy.wait_send()
    for turn_ in range(ITERS + 1):
        for share in range(SHARES):
            for o, f in partners:
                row_copy(turn_, share, o, f, turn_ == 0).wait_send()

    def drain_columns(o, carry):
        for it in range(ITERS):
            col_copy(it, o).wait_send()
        return carry

    lax.fori_loop(1, chips, drain_columns, 0)

    def drain_sums(step, carry):
        for lot in range(lot_count):
            for way in range(2):
                sum_copy(way, lot, step).wait_send()
        return carry

    lax.fori_loop(0, chips - 2, drain_sums, 0)
    for lot in range(lot_count):
        for way in range(2):
            for a in range(2):
                last_copy(way, lot, a).wait_send()
    own_copy_sum.wait_send()


def solution(mesh):
    ring, groups = mesh.shape["rows"], mesh.shape["cent"]

    def on_device(vectors, centroids):
        rows, width = vectors.shape
        depth, cols = centroids.shape
        p = plan(ring, rows, width, depth, cols)
        chips, half, block, lots = p["chips"], p["half"], p["block"], p["lots"]
        both = 2 * rows
        dma = pltpu.SemaphoreType.DMA
        vmem = pltpu.VMEM
        return pl.pallas_call(
            functools.partial(kernel, ring, groups, rows * ring, cols * groups),
            out_shape=jax.ShapeDtypeStruct((depth, cols), f32),
            in_specs=[pl.BlockSpec(memory_space=pl.ANY)] * 2,
            out_specs=pl.BlockSpec(memory_space=pltpu.VMEM),
            scratch_shapes=[
                vmem((depth, cols), bf16),
                vmem((width, half), bf16),
                vmem((both, width), bf16),
                vmem((width, both), bf16),
                vmem((half, both), f32),
                vmem((half, both), bf16),
                vmem((width, half), f32),
                vmem((p["chunk"], width), bf16),
                vmem((max(8, p["chunks"]), both), f32),
                vmem((max(8, p["chunks"]), both), f32),
                vmem((max(8, p["chunks"]), both), f32),
                vmem((8, both), f32),
                vmem((half, LANES), f32),
                vmem((half, LANES), f32),
                vmem((ITERS + 1, 2 * groups, 2, both), f32),
                vmem((ITERS, chips, 1, half), f32),
                vmem((chips - 1, block, half), bf16),
                vmem((chips - 2, block, half), bf16),
                vmem((2, depth, half), bf16),
                vmem((depth, half), f32),
                dma((2, p["steps"], 2)),
                dma((2, p["steps"], 2)),
                dma((2,)),
                dma((4,)),
                dma((ITERS + 1, SHARES, 2 * groups)),
                dma((ITERS + 1, SHARES, 2 * groups)),
                dma((ITERS, chips)),
                dma((ITERS, chips)),
                dma((chips - 2, 2, lots)),
                dma((chips - 2, 2, lots)),
                dma((2, 2, lots)),
                dma((2, 2, lots)),
                dma((2,)),
            ],
            compiler_params=pltpu.CompilerParams(
                collective_id=0, has_side_effects=True, vmem_limit_bytes=66 * 1000 * 1000),
        )(vectors, centroids)

    return jax.shard_map(
        on_device,
        mesh=mesh,
        in_specs=(P("rows", None), P("rows", "cent")),
        out_specs=P("rows", "cent"),
        check_vma=False,
    )
```
